32 devices in a mesh: mode: 8 (over y, x, core), orb: 4 (over z).
Axes of the slice: x: 2, y: 2, z: 4, core: 2. Of those that a mesh axis runs over, the one named last changes fastest.
Arguments:
- correlators: float32 [512, 2, 256, 256], P('mode', None, 'orb'), may hold values from -6 to 6
- density: float32 [2, 256, 256], P(None, 'orb'), may hold values from -6 to 6
- bare_hamiltonian: float32 [2, 256, 256], P(None, 'orb'), may hold values from -0.375 to 0.375
- coupling: float32 [512], P('mode'), may hold values from -0.25 to 0.25
- propagator: float32 [512, 512], P('mode'), may hold values from -0.25 to 0.25
Outputs:
- correlators_out: float32 [512, 2, 256, 256], P('mode', None, 'orb')
- density_out: float32 [2, 256, 256], P(None, 'orb')
The draws below stay inside these ranges and needn't reach their ends.
All inputs are finite; a program needn't handle non-finite values.
Results may differ from the reference program's by a relative error of at most 0.0001.
Values sent between devices are 32-bit elements; how exact they have to be, the bound alone decides.
No kernel may reach another device: no remote copies, remote signals or barrier semaphores. Data moves between devices by JAX's collectives and lax.ppermute only.
A program may use at most 128 MiB of HBM per device.

```python
import math
import jax
import jax.numpy as jnp
from jax import lax

MODES = 512
NO = 256


def levels(stream_key, dims, shards, least, largest):
    gain = 1.0
    for dim, blocks in shards:
        draws = jax.random.uniform(jax.random.fold_in(jax.random.fold_in(stream_key, 6), dim), (blocks,), jnp.float32, least / len(shards), largest / len(shards))
        gain = gain * jnp.repeat(jnp.exp(draws), dims[dim] // blocks).reshape((-1,) + (1,) * (len(dims) - 1 - dim))
    return gain


def noise(stream_key, shape, deviation, reach, split=(), held_as=jnp.bfloat16):
    gain = levels(stream_key, shape, split, -0.22, 0.18) if split else 1.0
    values = jax.random.normal(stream_key, shape, jnp.float32) * deviation * gain
    return jnp.minimum(jnp.maximum(values, -reach), reach).astype(held_as)


def setup_inputs(seed: int = 0) -> dict:
    arg_keys = jax.random.split(jax.random.key(seed), 6)
    return {
        "correlators": noise(arg_keys[0], (MODES, 2, NO, NO), 1.0, 6.0, ((0, 8), (2, 4)), jnp.float32),
        "density": noise(arg_keys[1], (2, NO, NO), 1.0, 6.0, ((1, 4),), jnp.float32),
        "bare_hamiltonian": noise(arg_keys[2], (2, NO, NO), NO ** -0.5, 0.375, ((1, 4),), jnp.float32),
        "coupling": noise(arg_keys[3], (MODES,), MODES ** -0.5, 0.25, ((0, 8),), jnp.float32),
        "propagator": noise(arg_keys[4], (MODES, MODES), MODES ** -0.5, 0.25, ((0, 8),), jnp.float32),
    }


time_step = 0.1
field_weight = 0.0625


def contract(form, first, second):
    return jnp.einsum(form, first, second, precision=lax.Precision.HIGHEST)


def left_product(matrix, stack):
    real = contract('ij,mjk->mik', matrix[0], stack[:, 0]) - contract('ij,mjk->mik', matrix[1], stack[:, 1])
    imag = contract('ij,mjk->mik', matrix[0], stack[:, 1]) + contract('ij,mjk->mik', matrix[1], stack[:, 0])
    return jnp.stack([real, imag], axis=1)


def right_product(stack, matrix):
    real = contract('mij,jk->mik', stack[:, 0], matrix[0]) - contract('mij,jk->mik', stack[:, 1], matrix[1])
    imag = contract('mij,jk->mik', stack[:, 0], matrix[1]) + contract('mij,jk->mik', stack[:, 1], matrix[0])
    return jnp.stack([real, imag], axis=1)


def reference(correlators, density, bare_hamiltonian, coupling, propagator):
    block = math.gcd(MODES, 64)

    def substep(stacks, dens, hamil):
        shaped = stacks.reshape(MODES // block, block, 2, NO, NO)
        weights = coupling.reshape(MODES // block, block)

        def advance(pair):
            stack, weight = pair
            commut = left_product(hamil, stack) - right_product(stack, hamil)
            turned = jnp.stack([commut[:, 1], -commut[:, 0]], axis=1)
            return stack + time_step * turned + time_step * weight[:, None, None, None] * dens[None]

        updated = lax.map(advance, (shaped, weights)).reshape(MODES, 2, NO, NO)
        collision = contract('m,mcij->cij', coupling, updated)
        dens = dens + time_step * collision
        return updated, dens, bare_hamiltonian + field_weight * dens

    hamil = bare_hamiltonian + field_weight * density
    stacks, dens = correlators, density
    for turn in range(2):
        stacks, dens, hamil = substep(stacks, dens, hamil)
    stacks = contract('mn,nx->mx', propagator, stacks.reshape(MODES, -1)).reshape(MODES, 2, NO, NO)
    stacks, dens, hamil = substep(stacks, dens, hamil)
    return stacks, dens
```

```python
import jax
import jax.numpy as jnp
from jax import lax
from jax.experimental import pallas as pl
from jax.experimental.pallas import tpu as pltpu
from jax.sharding import PartitionSpec as P

time_step = 0.1
field_weight = 0.0625
tile_rows, tile_cols = 8, 128
out_chunks = 4


def contract(form, first, second):
    return jnp.einsum(form, first, second, precision=lax.Precision.HIGHEST)


def embed(matrix):
    real, imag = matrix[0], matrix[1]
    return jnp.concatenate(
        [jnp.concatenate([real, -imag], axis=1), jnp.concatenate([imag, real], axis=1)], axis=0
    )


def product(first, second):
    flat = second.reshape(-1, second.shape[-1])
    return contract("ij,jk->ik", embed(first), flat).reshape(second.shape)


def generator(hamil):
    return jnp.stack([time_step * hamil[1], -time_step * hamil[0]])


def apply_step(gen, matrix):
    return matrix + product(gen, matrix) - product(matrix, gen)


def split(values):
    high = lax.reduce_precision(values, exponent_bits=8, mantissa_bits=7)
    return high.astype(jnp.bfloat16), (values - high).astype(jnp.bfloat16)


def split_in_kernel(values):
    high = values.astype(jnp.bfloat16)
    return high, (values - high.astype(jnp.float32)).astype(jnp.bfloat16)


def dot(first, second):
    return jnp.dot(first, second, preferred_element_type=jnp.float32)


def densities(dens, bare, coupled, norm):
    gen0 = generator(bare + field_weight * dens)
    coupled1 = apply_step(gen0, coupled) + time_step * norm * dens
    dens1 = dens + time_step * coupled1
    gen1 = generator(bare + field_weight * dens1)
    coupled2 = apply_step(gen1, coupled1) + time_step * norm * dens1
    dens2 = dens1 + time_step * coupled2
    gen2 = generator(bare + field_weight * dens2)
    source = apply_step(gen2, time_step * (apply_step(gen1, dens) + dens1))
    return (gen0, gen1, gen2), dens2, source


def last_density(gens, dens2, source, coupled_mixed, norm, norm_mixed):
    value = coupled_mixed
    for gen in gens:
        value = apply_step(gen, value)
    return dens2 + time_step * (value + norm_mixed * source + time_step * norm * dens2)


def swap(array, axis, offset):
    return lax.ppermute(array, axis, [(i, i ^ offset) for i in range(lax.axis_size(axis))])


def gather_by_doubling(array, axis):
    place = lax.axis_index(axis)
    offset, done, current = lax.axis_size(axis) // 2, 0, array
    while offset:
        other = swap(current, axis, offset)
        upper = (place & offset) != 0
        current = jnp.stack(
            [jnp.where(upper, other, current), jnp.where(upper, current, other)], axis=done
        )
        done, offset = done + 1, offset // 2
    return current.reshape((-1,) + array.shape)


def mix_kernel(place_ref, high_ref, low_ref, *refs):
    groups = len(refs) - 4
    pieces, (out_ref, sum_ref, xh_ref, xl_ref) = refs[:groups], refs[groups:]
    place = place_ref[0]
    count = pieces[0].shape[0] // tile_rows
    modes = groups * count
    for k, piece in enumerate(pieces):
        base = pl.multiple_of((place ^ k) * count, count)
        for q in range(tile_rows):
            high, low = split_in_kernel(piece[pl.ds(q, count, stride=tile_rows), :])
            xh_ref[pl.ds(base, count), q * tile_cols : (q + 1) * tile_cols] = high
            xl_ref[pl.ds(base, count), q * tile_cols : (q + 1) * tile_cols] = low
    xh, xl = xh_ref[...], xl_ref[...]
    mixed = dot(high_ref[...], xh) + dot(high_ref[...], xl) + dot(low_ref[...], xh)
    for q in range(tile_rows):
        part = mixed[:, q * tile_cols : (q + 1) * tile_cols]
        out_ref[pl.ds(q, modes, stride=tile_rows), :] = part[:modes]
        sum_ref[q : q + 1, :] = part[modes : modes + 1]


def mix(place, high, low, pieces):
    groups, length = len(pieces), pieces[0].shape[0]
    modes = groups * length // tile_rows
    return pl.pallas_call(
        mix_kernel,
        out_shape=(
            jax.ShapeDtypeStruct((groups * length, tile_cols), jnp.float32),
            jax.ShapeDtypeStruct((tile_rows, tile_cols), jnp.float32),
        ),
        in_specs=[pl.BlockSpec(memory_space=pltpu.SMEM)]
        + [pl.BlockSpec(memory_space=pltpu.VMEM)] * (2 + groups),
        out_specs=(
            pl.BlockSpec(memory_space=pltpu.VMEM),
            pl.BlockSpec(memory_space=pltpu.VMEM),
        ),
        scratch_shapes=[
            pltpu.VMEM((modes, tile_rows * tile_cols), jnp.bfloat16),
            pltpu.VMEM((modes, tile_rows * tile_cols), jnp.bfloat16),
        ],
        name="mix",
    )(place, high, low, *pieces)


def steps_kernel(groups, rings, blocks, place_ref, scale_ref, left_ref, right_ref, source_ref, dens_ref, *refs):
    pieces, outs, g_ref = refs[: len(blocks)], refs[len(blocks) : -1], refs[-1]
    order = g_ref.shape[-1]
    rows = order // rings
    half = groups // 2
    deep = 1 + max(b for b, _ in blocks)
    for piece, (b, h) in zip(pieces, blocks):
        for c in range(2):
            for d in range(half):
                for z in range(rings):
                    row = z * rows + (d * deep + b) * tile_rows
                    g_ref[c, row : row + tile_rows, h * tile_cols : (h + 1) * tile_cols] = piece[
                        (c * half + d) * rings + z
                    ]
    real, imag = g_ref[0], g_ref[1]
    for turn in range(left_ref.shape[0]):
        rh, rl = split_in_kernel(real)
        ih, il = split_in_kernel(imag)
        left = dot(left_ref[turn], jnp.concatenate([rh, ih, rl, il, rh, ih], axis=0))
        right = dot(jnp.concatenate([rh, ih, rl, il, rh, ih], axis=1), right_ref[turn])
        real = real + (left[:order] - right[:, :order])
        imag = imag + (left[order:] - right[:, order:])
    m = pl.program_id(0)
    mixed, own = scale_ref[0, m], scale_ref[1, m]
    g_ref[0] = real + mixed * source_ref[0] + own * dens_ref[0]
    g_ref[1] = imag + mixed * source_ref[1] + own * dens_ref[1]
    place = place_ref[0]
    for k, out in enumerate(outs):
        base = pl.multiple_of((place ^ k) * rows, rows)
        out[0] = g_ref[:, pl.ds(base, rows), :]


def steps(place, scales, left, right, source, dens, pieces, blocks, groups, rings, first, count):
    order = dens.shape[-1]
    rows = order // rings
    whole = pl.BlockSpec(memory_space=pltpu.VMEM)
    table = pl.BlockSpec(memory_space=pltpu.SMEM)
    return pl.pallas_call(
        lambda *refs: steps_kernel(groups, rings, blocks, *refs),
        grid=(count,),
        out_shape=tuple(
            jax.ShapeDtypeStruct((count, 2, rows, order), jnp.float32) for _ in range(rings)
        ),
        in_specs=[table, table, whole, whole, whole, whole]
        + [
            pl.BlockSpec((groups * rings, tile_rows, tile_cols), lambda m: (0, first + m, 0))
            for _ in pieces
        ],
        out_specs=tuple(
            pl.BlockSpec((1, 2, rows, order), lambda m: (m, 0, 0, 0)) for _ in range(rings)
        ),
        scratch_shapes=[pltpu.VMEM((2, order, order), jnp.float32)],
        name="steps",
    )(place, scales, left, right, source, dens, *pieces)


def triple(gens):
    lefts, rights = [], []
    for gen in gens:
        high, low = split(embed(gen))
        lefts.append(jnp.concatenate([high, high, low], axis=1))
        high, low = split(embed(jnp.stack([gen[0], -gen[1]])))
        rights.append(jnp.concatenate([high, high, low], axis=0))
    return jnp.stack(lefts), jnp.stack(rights)


def on_device(correlators, density, bare_hamiltonian, coupling, propagator):
    local, _, rows, order = correlators.shape
    groups, rings = lax.axis_size("mode"), lax.axis_size("orb")
    place, ring = lax.axis_index("mode"), lax.axis_index("orb")
    modes = local * groups
    owned = local // rings
    depth = 2 * rows // groups

    gathered = gather_by_doubling(
        jnp.concatenate(
            [propagator, jnp.zeros((tile_rows, modes), jnp.float32).at[0, :local].set(coupling)]
        ),
        "mode",
    )
    weights = gathered[:, local, :local].reshape(modes)
    full = gathered[:, :local].reshape(modes, modes)
    mixed_weights = contract("m,mn->n", weights, full)
    norm = jnp.sum(weights * weights)
    norm_mixed = jnp.sum(mixed_weights * weights)
    rows16 = jnp.zeros((2 * tile_rows, modes), jnp.float32).at[0].set(mixed_weights)
    high, low = split(jnp.concatenate([full, rows16]))

    flat = correlators.reshape(local, 2 * rows, order)
    deep, wide = depth // tile_rows, order // tile_cols
    blocks = [(b, h) for b in range(deep) for h in range(wide)]
    wholes, sums = [], {}
    for b, h in blocks:
        pieces = []
        for k in range(groups):
            start = (0, (place ^ k) * depth + b * tile_rows, h * tile_cols)
            piece = lax.dynamic_slice(flat, start, (local, tile_rows, tile_cols))
            piece = piece.reshape(local * tile_rows, tile_cols)
            pieces.append(swap(piece, "mode", k) if k else piece)
        mixed, sums[b, h] = mix(place.reshape(1), high, low, pieces)
        mixed = mixed.reshape(groups * rings, owned * tile_rows, tile_cols)
        wholes.append(lax.all_to_all(mixed, ("mode", "orb"), 0, 0, tiled=True))

    both = lax.all_gather(jnp.stack([density, bare_hamiltonian]), "orb", axis=2, tiled=True)
    coupled = lax.psum(contract("m,mcij->cij", coupling, correlators), "mode")
    coupled = lax.all_gather(coupled, "orb", axis=1, tiled=True)
    gens, dens2, source = densities(both[0], both[1], coupled, norm)
    left, right = triple(gens)
    own_coupling = lax.dynamic_slice_in_dim(coupling, ring * owned, owned, 0)
    own_rows = lax.dynamic_slice_in_dim(propagator, ring * owned, owned, 0)
    scales = jnp.stack([contract("mn,n->m", own_rows, weights), time_step * own_coupling])

    chunk = owned // out_chunks
    stacks = jnp.zeros(correlators.shape, jnp.float32)
    for turn in range(out_chunks):
        first = turn * chunk
        parts = steps(
            ring.reshape(1), scales[:, first : first + chunk], left, right, source, dens2,
            wholes, blocks, groups, rings, first, chunk,
        )
        for k, part in enumerate(parts):
            part = swap(part, "orb", k) if k else part
            stacks = lax.dynamic_update_slice(stacks, part, ((ring ^ k) * owned + first, 0, 0, 0))

    summed = jnp.concatenate(
        [jnp.concatenate([sums[b, h] for h in range(wide)], axis=1) for b in range(deep)], axis=0
    )
    summed = lax.all_gather(summed, ("mode", "orb"), axis=0).reshape(2, groups // 2, rings, depth, order)
    coupled_mixed = summed.transpose(0, 2, 1, 3, 4).reshape(2, order, order)
    dens = last_density(gens, dens2, source, coupled_mixed, norm, norm_mixed)
    return stacks, lax.dynamic_slice_in_dim(dens, ring * rows, rows, 1)


def on_device_plain(correlators, density, bare_hamiltonian, coupling, propagator):
    local, _, rows, order = correlators.shape
    groups, rings = lax.axis_size("mode"), lax.axis_size("orb")
    ring = lax.axis_index("orb")
    owned = local // rings
    full = lax.all_gather(propagator, "mode", axis=0, tiled=True)
    weights = lax.all_gather(coupling, "mode", axis=0, tiled=True)
    mixed_weights = contract("m,mn->n", weights, full)
    norm, norm_mixed = jnp.sum(weights * weights), jnp.sum(mixed_weights * weights)
    both = lax.all_gather(jnp.stack([density, bare_hamiltonian]), "orb", axis=2, tiled=True)
    sums = jnp.stack(
        [
            contract("m,mcij->cij", coupling, correlators),
            contract(
                "m,mcij->cij",
                lax.dynamic_slice_in_dim(mixed_weights, lax.axis_index("mode") * local, local, 0),
                correlators,
            ),
        ]
    )
    sums = lax.all_gather(lax.psum(sums, "mode"), "orb", axis=2, tiled=True)
    gens, dens2, source = densities(both[0], both[1], sums[0], norm)
    entries = lax.all_to_all(correlators.reshape(local, groups, -1), "mode", 1, 0, tiled=True)
    mixed = contract("mn,nx->mx", full, entries.reshape(full.shape[0], -1))
    mixed = lax.all_to_all(mixed.reshape(groups * rings, -1), ("mode", "orb"), 0, 0, tiled=True)
    whole = mixed.reshape(groups, rings, owned, -1).transpose(2, 1, 0, 3)
    whole = whole.reshape(owned, rings, 2, rows, order).transpose(0, 2, 1, 3, 4)
    whole = whole.reshape(owned, 2, order, order)
    for gen in gens:
        whole = jax.vmap(lambda matrix, gen=gen: apply_step(gen, matrix))(whole)
    own_coupling = lax.dynamic_slice_in_dim(coupling, ring * owned, owned, 0)
    own_rows = lax.dynamic_slice_in_dim(propagator, ring * owned, owned, 0)
    scale = contract("mn,n->m", own_rows, weights)
    whole = (
        whole
        + scale[:, None, None, None] * source[None]
        + time_step * own_coupling[:, None, None, None] * dens2[None]
    )
    stacks = lax.all_to_all(whole, "orb", split_axis=2, concat_axis=0, tiled=True)
    dens = last_density(gens, dens2, source, sums[1], norm, norm_mixed)
    return stacks, lax.dynamic_slice_in_dim(dens, ring * rows, rows, 1)


def solution(mesh):
    in_specs = (
        P("mode", None, "orb", None),
        P(None, "orb", None),
        P(None, "orb", None),
        P("mode"),
        P("mode", None),
    )
    out_specs = (P("mode", None, "orb", None), P(None, "orb", None))
    groups, rings = mesh.shape["mode"], mesh.shape["orb"]

    def body(correlators, *others):
        local, _, rows, order = correlators.shape
        fits = (
            groups > 1
            and groups & (groups - 1) == 0
            and rings & (rings - 1) == 0
            and 2 * rows % (groups * tile_rows) == 0
            and order % tile_cols == 0
            and local % (2 * tile_rows) == 0
            and local % (rings * out_chunks) == 0
        )
        return (on_device if fits else on_device_plain)(correlators, *others)

    return jax.shard_map(
        body, mesh=mesh, in_specs=in_specs, out_specs=out_specs, check_vma=False
    )
```

```python
import jax
import jax.numpy as jnp
from jax import lax
from jax.experimental import pallas as pl
from jax.experimental.pallas import tpu as pltpu
from jax.sharding import PartitionSpec as P

time_step = 0.1
field_weight = 0.0625
tile_rows, tile_cols = 8, 128
out_shares = (1, 3, 6, 6)


def contract(form, first, second):
    return jnp.einsum(form, first, second, precision=lax.Precision.HIGHEST)


def embed(matrix):
    real, imag = matrix[0], matrix[1]
    return jnp.concatenate(
        [jnp.concatenate([real, -imag], axis=1), jnp.concatenate([imag, real], axis=1)], axis=0
    )


def product(first, second):
    flat = second.reshape(-1, second.shape[-1])
    return contract("ij,jk->ik", embed(first), flat).reshape(second.shape)


def generator(hamil):
    return jnp.stack([time_step * hamil[1], -time_step * hamil[0]])


def apply_step(gen, matrix):
    return matrix + product(gen, matrix) - product(matrix, gen)


def split(values):
    high = lax.reduce_precision(values, exponent_bits=8, mantissa_bits=7)
    return high.astype(jnp.bfloat16), (values - high).astype(jnp.bfloat16)


def split_in_kernel(values):
    high = values.astype(jnp.bfloat16)
    return high, (values - high.astype(jnp.float32)).astype(jnp.bfloat16)


def dot(first, second):
    return jnp.dot(first, second, preferred_element_type=jnp.float32)


def densities(dens, bare, coupled, norm):
    gen0 = generator(bare + field_weight * dens)
    coupled1 = apply_step(gen0, coupled) + time_step * norm * dens
    dens1 = dens + time_step * coupled1
    gen1 = generator(bare + field_weight * dens1)
    coupled2 = apply_step(gen1, coupled1) + time_step * norm * dens1
    dens2 = dens1 + time_step * coupled2
    gen2 = generator(bare + field_weight * dens2)
    source = apply_step(gen2, time_step * (apply_step(gen1, dens) + dens1))
    return (gen0, gen1, gen2), dens2, source


def last_density(gens, dens2, source, coupled_mixed, norm, norm_mixed):
    value = coupled_mixed
    for gen in gens:
        value = apply_step(gen, value)
    return dens2 + time_step * (value + norm_mixed * source + time_step * norm * dens2)


def swap(array, axis, offset):
    return lax.ppermute(array, axis, [(i, i ^ offset) for i in range(lax.axis_size(axis))])


def gather_by_doubling(array, axis, gate=None):
    place = lax.axis_index(axis)
    offset, done, current = lax.axis_size(axis) // 2, 0, array
    while offset:
        other = swap(current, axis, offset)
        if gate is not None and not done:
            other = after(other, gate)
        upper = (place & offset) != 0
        current = jnp.stack(
            [jnp.where(upper, other, current), jnp.where(upper, current, other)], axis=done
        )
        done, offset = done + 1, offset // 2
    return current.reshape((-1,) + array.shape)


def exchange(pieces, axis):
    return [swap(piece, axis, k) if k else piece for k, piece in enumerate(pieces)]


def by_place(received, place):
    current, offset = jnp.stack(received), 1
    while offset < len(received):
        pairs = current.reshape((-1, 2, offset) + received[0].shape)
        turned = jnp.concatenate([pairs[:, 1:], pairs[:, :1]], axis=1)
        current = jnp.where((place & offset) != 0, turned, pairs)
        offset *= 2
    return current.reshape((len(received),) + received[0].shape)


def after(array, other):
    return lax.optimization_barrier((array, other))[0]


def pack_kernel(depth, b, h, place_ref, flat_ref, *refs):
    outs, (held_ref, into, back) = refs[:-3], refs[-3:]
    fetched, stored = [], []
    for k, out in enumerate(outs):
        row = pl.multiple_of((place_ref[0] ^ k) * depth + b * tile_rows, tile_rows)
        source = flat_ref.at[:, pl.ds(row, tile_rows), h * tile_cols : (h + 1) * tile_cols]
        fetched.append(pltpu.make_async_copy(source, held_ref.at[k], into.at[k]))
        stored.append(pltpu.make_async_copy(held_ref.at[k], out, back.at[k]))
        fetched[-1].start()
    for fetch, store in zip(fetched, stored):
        fetch.wait()
        store.start()
    for store in stored:
        store.wait()


def pack(place, flat, groups, depth, b, h):
    piece = jax.ShapeDtypeStruct((flat.shape[0], tile_rows, tile_cols), jnp.float32)
    return pl.pallas_call(
        lambda *refs: pack_kernel(depth, b, h, *refs),
        out_shape=(piece,) * groups,
        in_specs=[pl.BlockSpec(memory_space=pltpu.SMEM), pl.BlockSpec(memory_space=pl.ANY)],
        out_specs=(pl.BlockSpec(memory_space=pl.ANY),) * groups,
        scratch_shapes=[
            pltpu.VMEM((groups,) + piece.shape, jnp.float32),
            pltpu.SemaphoreType.DMA((groups,)),
            pltpu.SemaphoreType.DMA((groups,)),
        ],
        name="pack",
    )(place, flat)


def mix_kernel(place_ref, high_ref, low_ref, *refs):
    groups = len(refs) - 4
    pieces, (out_ref, sum_ref, xh_ref, xl_ref) = refs[:groups], refs[groups:]
    place = place_ref[0]
    count = pieces[0].shape[0] // tile_rows
    modes = groups * count
    for k, piece in enumerate(pieces):
        base = pl.multiple_of((place ^ k) * count, count)
        for q in range(tile_rows):
            high, low = split_in_kernel(piece[pl.ds(q, count, stride=tile_rows), :])
            xh_ref[pl.ds(base, count), q * tile_cols : (q + 1) * tile_cols] = high
            xl_ref[pl.ds(base, count), q * tile_cols : (q + 1) * tile_cols] = low
    xh, xl = xh_ref[...], xl_ref[...]
    mixed = dot(high_ref[...], xh) + dot(high_ref[...], xl) + dot(low_ref[...], xh)
    for q in range(tile_rows):
        part = mixed[:, q * tile_cols : (q + 1) * tile_cols]
        out_ref[pl.ds(q, modes, stride=tile_rows), :] = part[:modes]
        sum_ref[q : q + 1, :] = part[modes : modes + 1]


def mix(place, high, low, pieces):
    groups, length = len(pieces), pieces[0].shape[0]
    modes = groups * length // tile_rows
    return pl.pallas_call(
        mix_kernel,
        out_shape=(
            jax.ShapeDtypeStruct((groups * length, tile_cols), jnp.float32),
            jax.ShapeDtypeStruct((tile_rows, tile_cols), jnp.float32),
        ),
        in_specs=[pl.BlockSpec(memory_space=pltpu.SMEM)]
        + [pl.BlockSpec(memory_space=pltpu.VMEM)] * (2 + groups),
        out_specs=(
            pl.BlockSpec(memory_space=pltpu.VMEM),
            pl.BlockSpec(memory_space=pltpu.VMEM),
        ),
        scratch_shapes=[
            pltpu.VMEM((modes, tile_rows * tile_cols), jnp.bfloat16),
            pltpu.VMEM((modes, tile_rows * tile_cols), jnp.bfloat16),
        ],
        name="mix",
    )(place, high, low, *pieces)


def steps_kernel(groups, rings, blocks, place_ref, scale_ref, left_ref, right_ref, source_ref, dens_ref, *refs):
    pieces, outs, g_ref = refs[: len(blocks)], refs[len(blocks) : -1], refs[-1]
    order = g_ref.shape[-1]
    rows = order // rings
    half = groups // 2
    deep = 1 + max(b for b, _ in blocks)
    for piece, (b, h) in zip(pieces, blocks):
        for c in range(2):
            for d in range(half):
                for z in range(rings):
                    row = z * rows + (d * deep + b) * tile_rows
                    g_ref[c, row : row + tile_rows, h * tile_cols : (h + 1) * tile_cols] = piece[
                        (c * half + d) * rings + z
                    ]
    def turn_step(turn, _):
        real, imag = g_ref[0], g_ref[1]
        rh, rl = split_in_kernel(real)
        ih, il = split_in_kernel(imag)
        left = dot(left_ref[turn], jnp.concatenate([rh, ih, rl, il, rh, ih], axis=0))
        right = dot(jnp.concatenate([rh, ih, rl, il, rh, ih], axis=1), right_ref[turn])
        g_ref[0] = real + (left[:order] - right[:, :order])
        g_ref[1] = imag + (left[order:] - right[:, order:])
        return 0

    lax.fori_loop(0, left_ref.shape[0], turn_step, 0)
    m = pl.program_id(0)
    mixed, own = scale_ref[0, m], scale_ref[1, m]
    g_ref[0] = g_ref[0] + mixed * source_ref[0] + own * dens_ref[0]
    g_ref[1] = g_ref[1] + mixed * source_ref[1] + own * dens_ref[1]
    place = place_ref[0]
    for k, out in enumerate(outs):
        base = pl.multiple_of((place ^ k) * rows, rows)
        out[0] = g_ref[:, pl.ds(base, rows), :]


def steps(place, scales, left, right, source, dens, pieces, blocks, groups, rings, first, count):
    order = dens.shape[-1]
    rows = order // rings
    whole = pl.BlockSpec(memory_space=pltpu.VMEM)
    table = pl.BlockSpec(memory_space=pltpu.SMEM)
    return pl.pallas_call(
        lambda *refs: steps_kernel(groups, rings, blocks, *refs),
        grid=(count,),
        out_shape=tuple(
            jax.ShapeDtypeStruct((count, 2, rows, order), jnp.float32) for _ in range(rings)
        ),
        in_specs=[table, table, whole, whole, whole, whole]
        + [
            pl.BlockSpec((groups * rings, tile_rows, tile_cols), lambda m: (0, first + m, 0))
            for _ in pieces
        ],
        out_specs=tuple(
            pl.BlockSpec((1, 2, rows, order), lambda m: (m, 0, 0, 0)) for _ in range(rings)
        ),
        scratch_shapes=[pltpu.VMEM((2, order, order), jnp.float32)],
        name="steps",
    )(place, scales, left, right, source, dens, *pieces)


def triple(gens):
    lefts, rights = [], []
    for gen in gens:
        high, low = split(embed(gen))
        lefts.append(jnp.concatenate([high, high, low], axis=1))
        high, low = split(embed(jnp.stack([gen[0], -gen[1]])))
        rights.append(jnp.concatenate([high, high, low], axis=0))
    return jnp.stack(lefts), jnp.stack(rights)


def on_device(correlators, density, bare_hamiltonian, coupling, propagator):
    local, _, rows, order = correlators.shape
    groups, rings = lax.axis_size("mode"), lax.axis_size("orb")
    place, ring = lax.axis_index("mode"), lax.axis_index("orb")
    modes = local * groups
    owned = local // rings
    depth = 2 * rows // groups

    flat = correlators.reshape(local, 2 * rows, order)
    deep, wide = depth // tile_rows, order // tile_cols
    blocks = [(b, h) for b in range(deep) for h in range(wide)]
    here = place.reshape(1)
    packed = pack(here, flat, groups, depth, *blocks[0])

    gathered = gather_by_doubling(
        jnp.concatenate(
            [propagator, jnp.zeros((tile_rows, modes), jnp.float32).at[0, :local].set(coupling)]
        ),
        "mode",
        packed[0],
    )
    weights = gathered[:, local, :local].reshape(modes)
    full = gathered[:, :local].reshape(modes, modes)
    mixed_weights = contract("m,mn->n", weights, full)
    norm = jnp.sum(weights * weights)
    norm_mixed = jnp.sum(mixed_weights * weights)
    rows16 = jnp.zeros((2 * tile_rows, modes), jnp.float32).at[0].set(mixed_weights)
    high, low = split(jnp.concatenate([full, rows16]))

    both = gather_by_doubling(jnp.stack([density, bare_hamiltonian]), "orb")
    both = jnp.moveaxis(both, 0, 2).reshape(2, 2, order, order)

    share = rows // groups
    coupled = jnp.sum(coupling[:, None, None, None] * correlators, axis=0)
    coupled = exchange(
        [
            lax.dynamic_slice_in_dim(coupled, (place ^ k) * share, share, 1)
            for k in range(groups)
        ],
        "mode",
    )
    wholes, sums, mixes, last = [], {}, [], packed
    for turn, (b, h) in enumerate(blocks):
        if turn:
            gates = (mixes[max(turn - 2, 0)], last[0])
            packed = last = pack(here, after(flat, gates), groups, depth, b, h)
        pieces = exchange([piece.reshape(-1, tile_cols) for piece in packed], "mode")
        gates = (both, tuple(coupled)) if not turn else tuple(wholes[turn - 2 : turn - 1])
        mixed, sums[b, h] = mix(after(here, gates), high, low, pieces)
        mixes.append(mixed)
        mixed = mixed.reshape(groups * rings, owned * tile_rows, tile_cols)
        wholes.append(lax.all_to_all(mixed, ("mode", "orb"), 0, 0, tiled=True))

    coupled = sum(coupled)
    coupled = exchange([after(coupled, mixes[0])] * rings, "orb")
    coupled = by_place(after(tuple(coupled), mixes[min(1, len(mixes) - 1)]), ring)
    coupled = exchange([coupled] * groups, "mode")
    coupled = by_place(after(tuple(coupled), mixes[min(2, len(mixes) - 1)]), place)
    coupled = coupled.transpose(2, 1, 0, 3, 4).reshape(2, order, order)
    gens, dens2, source = densities(both[0], both[1], coupled, norm)
    left, right = triple(gens)
    own_coupling = lax.dynamic_slice_in_dim(coupling, ring * owned, owned, 0)
    own_rows = lax.dynamic_slice_in_dim(propagator, ring * owned, owned, 0)
    scales = jnp.stack([contract("mn,n->m", own_rows, weights), time_step * own_coupling])

    stacks = jnp.zeros(correlators.shape, jnp.float32)
    first, finished = 0, []
    for share in out_shares:
        chunk = share * owned // sum(out_shares)
        parts = steps(
            ring.reshape(1), scales[:, first : first + chunk], left, right, source, dens2,
            wholes, blocks, groups, rings, first, chunk,
        )
        finished.append(parts[0])
        for k, part in enumerate(parts):
            part = swap(part, "orb", k) if k else part
            stacks = lax.dynamic_update_slice(stacks, part, ((ring ^ k) * owned + first, 0, 0, 0))
        first += chunk

    summed = jnp.concatenate(
        [jnp.concatenate([sums[b, h] for h in range(wide)], axis=1) for b in range(deep)], axis=0
    )
    summed = gather_by_doubling(after(summed, finished[0]), "orb")
    summed = gather_by_doubling(after(summed, finished[-1]), "mode")
    summed = summed.reshape(2, groups // 2, rings, depth, order).transpose(0, 2, 1, 3, 4)
    coupled_mixed = summed.reshape(2, order, order)
    dens = last_density(gens, dens2, source, coupled_mixed, norm, norm_mixed)
    return stacks, lax.dynamic_slice_in_dim(dens, ring * rows, rows, 1)


def on_device_plain(correlators, density, bare_hamiltonian, coupling, propagator):
    local, _, rows, order = correlators.shape
    groups, rings = lax.axis_size("mode"), lax.axis_size("orb")
    ring = lax.axis_index("orb")
    owned = local // rings
    full = lax.all_gather(propagator, "mode", axis=0, tiled=True)
    weights = lax.all_gather(coupling, "mode", axis=0, tiled=True)
    mixed_weights = contract("m,mn->n", weights, full)
    norm, norm_mixed = jnp.sum(weights * weights), jnp.sum(mixed_weights * weights)
    both = lax.all_gather(jnp.stack([density, bare_hamiltonian]), "orb", axis=2, tiled=True)
    sums = jnp.stack(
        [
            contract("m,mcij->cij", coupling, correlators),
            contract(
                "m,mcij->cij",
                lax.dynamic_slice_in_dim(mixed_weights, lax.axis_index("mode") * local, local, 0),
                correlators,
            ),
        ]
    )
    sums = lax.all_gather(lax.psum(sums, "mode"), "orb", axis=2, tiled=True)
    gens, dens2, source = densities(both[0], both[1], sums[0], norm)
    entries = lax.all_to_all(correlators.reshape(local, groups, -1), "mode", 1, 0, tiled=True)
    mixed = contract("mn,nx->mx", full, entries.reshape(full.shape[0], -1))
    mixed = lax.all_to_all(mixed.reshape(groups * rings, -1), ("mode", "orb"), 0, 0, tiled=True)
    whole = mixed.reshape(groups, rings, owned, -1).transpose(2, 1, 0, 3)
    whole = whole.reshape(owned, rings, 2, rows, order).transpose(0, 2, 1, 3, 4)
    whole = whole.reshape(owned, 2, order, order)
    for gen in gens:
        whole = jax.vmap(lambda matrix, gen=gen: apply_step(gen, matrix))(whole)
    own_coupling = lax.dynamic_slice_in_dim(coupling, ring * owned, owned, 0)
    own_rows = lax.dynamic_slice_in_dim(propagator, ring * owned, owned, 0)
    scale = contract("mn,n->m", own_rows, weights)
    whole = (
        whole
        + scale[:, None, None, None] * source[None]
        + time_step * own_coupling[:, None, None, None] * dens2[None]
    )
    stacks = lax.all_to_all(whole, "orb", split_axis=2, concat_axis=0, tiled=True)
    dens = last_density(gens, dens2, source, sums[1], norm, norm_mixed)
    return stacks, lax.dynamic_slice_in_dim(dens, ring * rows, rows, 1)


def solution(mesh):
    in_specs = (
        P("mode", None, "orb", None),
        P(None, "orb", None),
        P(None, "orb", None),
        P("mode"),
        P("mode", None),
    )
    out_specs = (P("mode", None, "orb", None), P(None, "orb", None))
    groups, rings = mesh.shape["mode"], mesh.shape["orb"]

    def body(correlators, *others):
        local, _, rows, order = correlators.shape
        fits = (
            groups > 1
            and groups & (groups - 1) == 0
            and rings & (rings - 1) == 0
            and rows % (groups * tile_rows) == 0
            and order % tile_cols == 0
            and local % (2 * tile_rows) == 0
            and local % (rings * sum(out_shares)) == 0
        )
        return (on_device if fits else on_device_plain)(correlators, *others)

    return jax.shard_map(
        body, mesh=mesh, in_specs=in_specs, out_specs=out_specs, check_vma=False
    )
```

```python
import jax
import jax.numpy as jnp
from jax import lax
from jax.experimental import pallas as pl
from jax.experimental.pallas import tpu as pltpu
from jax.sharding import PartitionSpec as P

time_step = 0.1
field_weight = 0.0625
tile_rows, tile_cols = 8, 128
out_shares = (1, 3, 6, 6)


def contract(form, first, second):
    return jnp.einsum(form, first, second, precision=lax.Precision.HIGHEST)


def embed(matrix):
    real, imag = matrix[0], matrix[1]
    return jnp.concatenate(
        [jnp.concatenate([real, -imag], axis=1), jnp.concatenate([imag, real], axis=1)], axis=0
    )


def product(first, second):
    flat = second.reshape(-1, second.shape[-1])
    return contract("ij,jk->ik", embed(first), flat).reshape(second.shape)


def generator(hamil):
    return jnp.stack([time_step * hamil[1], -time_step * hamil[0]])


def apply_step(gen, matrix):
    return matrix + product(gen, matrix) - product(matrix, gen)


def split(values):
    high = lax.reduce_precision(values, exponent_bits=8, mantissa_bits=7)
    return high.astype(jnp.bfloat16), (values - high).astype(jnp.bfloat16)


def split_in_kernel(values):
    high = values.astype(jnp.bfloat16)
    return high, (values - high.astype(jnp.float32)).astype(jnp.bfloat16)


def dot(first, second):
    return jnp.dot(first, second, preferred_element_type=jnp.float32)


def densities(dens, bare, coupled, norm):
    gen0 = generator(bare + field_weight * dens)
    coupled1 = apply_step(gen0, coupled) + time_step * norm * dens
    dens1 = dens + time_step * coupled1
    gen1 = generator(bare + field_weight * dens1)
    coupled2 = apply_step(gen1, coupled1) + time_step * norm * dens1
    dens2 = dens1 + time_step * coupled2
    gen2 = generator(bare + field_weight * dens2)
    source = apply_step(gen2, time_step * (apply_step(gen1, dens) + dens1))
    return (gen0, gen1, gen2), dens2, source


def last_density(gens, dens2, source, coupled_mixed, norm, norm_mixed):
    value = coupled_mixed
    for gen in gens:
        value = apply_step(gen, value)
    return dens2 + time_step * (value + norm_mixed * source + time_step * norm * dens2)


def swap(array, axis, offset):
    return lax.ppermute(array, axis, [(i, i ^ offset) for i in range(lax.axis_size(axis))])


def gather_by_doubling(array, axis):
    place = lax.axis_index(axis)
    offset, done, current = lax.axis_size(axis) // 2, 0, array
    while offset:
        other = swap(current, axis, offset)
        upper = (place & offset) != 0
        current = jnp.stack(
            [jnp.where(upper, other, current), jnp.where(upper, current, other)], axis=done
        )
        done, offset = done + 1, offset // 2
    return current.reshape((-1,) + array.shape)


def exchange(pieces, axis):
    return [swap(piece, axis, k) if k else piece for k, piece in enumerate(pieces)]


def by_place(received, place):
    current, offset = jnp.stack(received), 1
    while offset < len(received):
        pairs = current.reshape((-1, 2, offset) + received[0].shape)
        turned = jnp.concatenate([pairs[:, 1:], pairs[:, :1]], axis=1)
        current = jnp.where((place & offset) != 0, turned, pairs)
        offset *= 2
    return current.reshape((len(received),) + received[0].shape)


def after(array, other):
    return lax.optimization_barrier((array, other))[0]


def pack_kernel(depth, b, h, place_ref, flat_ref, *refs):
    outs, (held_ref, into, back) = refs[:-3], refs[-3:]
    fetched, stored = [], []
    for k, out in enumerate(outs):
        row = pl.multiple_of((place_ref[0] ^ k) * depth + b * tile_rows, tile_rows)
        source = flat_ref.at[:, pl.ds(row, tile_rows), h * tile_cols : (h + 1) * tile_cols]
        fetched.append(pltpu.make_async_copy(source, held_ref.at[k], into.at[k]))
        stored.append(pltpu.make_async_copy(held_ref.at[k], out, back.at[k]))
        fetched[-1].start()
    for fetch, store in zip(fetched, stored):
        fetch.wait()
        store.start()
    for store in stored:
        store.wait()


def pack(place, flat, groups, depth, b, h):
    piece = jax.ShapeDtypeStruct((flat.shape[0], tile_rows, tile_cols), jnp.float32)
    return pl.pallas_call(
        lambda *refs: pack_kernel(depth, b, h, *refs),
        out_shape=(piece,) * groups,
        in_specs=[pl.BlockSpec(memory_space=pltpu.SMEM), pl.BlockSpec(memory_space=pl.ANY)],
        out_specs=(pl.BlockSpec(memory_space=pl.ANY),) * groups,
        scratch_shapes=[
            pltpu.VMEM((groups,) + piece.shape, jnp.float32),
            pltpu.SemaphoreType.DMA((groups,)),
            pltpu.SemaphoreType.DMA((groups,)),
        ],
        name="pack",
    )(place, flat)


def mix_kernel(place_ref, high_ref, low_ref, *refs):
    groups = len(refs) - 4
    pieces, (out_ref, sum_ref, xh_ref, xl_ref) = refs[:groups], refs[groups:]
    place = place_ref[0]
    count = pieces[0].shape[0] // tile_rows
    modes = groups * count
    for k, piece in enumerate(pieces):
        base = pl.multiple_of((place ^ k) * count, count)
        for q in range(tile_rows):
            high, low = split_in_kernel(piece[pl.ds(q, count, stride=tile_rows), :])
            xh_ref[pl.ds(base, count), q * tile_cols : (q + 1) * tile_cols] = high
            xl_ref[pl.ds(base, count), q * tile_cols : (q + 1) * tile_cols] = low
    xh, xl = xh_ref[...], xl_ref[...]
    mixed = dot(high_ref[...], xh) + dot(high_ref[...], xl) + dot(low_ref[...], xh)
    for q in range(tile_rows):
        part = mixed[:, q * tile_cols : (q + 1) * tile_cols]
        out_ref[pl.ds(q, modes, stride=tile_rows), :] = part[:modes]
        sum_ref[q : q + 1, :] = part[modes : modes + 1]


def mix(place, high, low, pieces):
    groups, length = len(pieces), pieces[0].shape[0]
    modes = groups * length // tile_rows
    return pl.pallas_call(
        mix_kernel,
        out_shape=(
            jax.ShapeDtypeStruct((groups * length, tile_cols), jnp.float32),
            jax.ShapeDtypeStruct((tile_rows, tile_cols), jnp.float32),
        ),
        in_specs=[pl.BlockSpec(memory_space=pltpu.SMEM)]
        + [pl.BlockSpec(memory_space=pltpu.VMEM)] * (2 + groups),
        out_specs=(
            pl.BlockSpec(memory_space=pltpu.VMEM),
            pl.BlockSpec(memory_space=pltpu.VMEM),
        ),
        scratch_shapes=[
            pltpu.VMEM((modes, tile_rows * tile_cols), jnp.bfloat16),
            pltpu.VMEM((modes, tile_rows * tile_cols), jnp.bfloat16),
        ],
        name="mix",
    )(place, high, low, *pieces)


def step_of(real, imag, left, right):
    order = real.shape[-1]
    rh, rl = split_in_kernel(real)
    ih, il = split_in_kernel(imag)
    before = dot(left, jnp.concatenate([rh, ih, rl, il, rh, ih], axis=0))
    behind = dot(jnp.concatenate([rh, ih, rl, il, rh, ih], axis=1), right)
    return (
        real + (before[:order] - behind[:, :order]),
        imag + (before[order:] - behind[:, order:]),
    )


def steps_kernel(groups, rings, blocks, place_ref, scale_ref, left_ref, right_ref, source_ref, dens_ref, *refs):
    pieces, outs = refs[: len(blocks)], refs[len(blocks) : -4]
    g_ref, left_held, right_held, sem = refs[-4:]
    order = g_ref.shape[-1]
    rows = order // rings
    half = groups // 2
    deep = 1 + max(b for b, _ in blocks)
    turns = left_ref.shape[0]
    m = pl.program_id(0)

    def fetch(turn):
        return (
            pltpu.make_async_copy(left_ref.at[turn], left_held.at[turn], sem.at[turn, 0]),
            pltpu.make_async_copy(right_ref.at[turn], right_held.at[turn], sem.at[turn, 1]),
        )

    @pl.when(m == 0)
    def _():
        for turn in range(turns):
            for copy in fetch(turn):
                copy.start()

    for piece, (b, h) in zip(pieces, blocks):
        for c in range(2):
            for d in range(half):
                for z in range(rings):
                    row = z * rows + (d * deep + b) * tile_rows
                    g_ref[c, row : row + tile_rows, h * tile_cols : (h + 1) * tile_cols] = piece[
                        (c * half + d) * rings + z
                    ]

    def turn_step(turn, _):
        @pl.when(m == 0)
        def _():
            for copy in fetch(turn):
                copy.wait()

        real, imag = step_of(g_ref[0], g_ref[1], left_held[turn], right_held[turn])
        g_ref[0] = real
        g_ref[1] = imag
        return 0

    lax.fori_loop(0, turns, turn_step, 0)
    mixed, own = scale_ref[0, m], scale_ref[1, m]
    g_ref[...] = g_ref[...] + mixed * source_ref[...] + own * dens_ref[...]
    place = place_ref[0]
    for k, out in enumerate(outs):
        base = pl.multiple_of((place ^ k) * rows, rows)
        out[0] = g_ref[:, pl.ds(base, rows), :]


def steps(place, scales, left, right, source, dens, pieces, blocks, groups, rings, first, count):
    order = dens.shape[-1]
    rows = order // rings
    whole = pl.BlockSpec(memory_space=pltpu.VMEM)
    table = pl.BlockSpec(memory_space=pltpu.SMEM)
    apart = pl.BlockSpec(memory_space=pl.ANY)
    return pl.pallas_call(
        lambda *refs: steps_kernel(groups, rings, blocks, *refs),
        grid=(count,),
        out_shape=tuple(
            jax.ShapeDtypeStruct((count, 2, rows, order), jnp.float32) for _ in range(rings)
        ),
        in_specs=[table, table, apart, apart, whole, whole]
        + [
            pl.BlockSpec((groups * rings, tile_rows, tile_cols), lambda m: (0, first + m, 0))
            for _ in pieces
        ],
        out_specs=tuple(
            pl.BlockSpec((1, 2, rows, order), lambda m: (m, 0, 0, 0)) for _ in range(rings)
        ),
        scratch_shapes=[
            pltpu.VMEM((2, order, order), jnp.float32),
            pltpu.VMEM(left.shape, left.dtype),
            pltpu.VMEM(right.shape, right.dtype),
            pltpu.SemaphoreType.DMA((left.shape[0], 2)),
        ],
        name="steps",
    )(place, scales, left, right, source, dens, *pieces)


def densities_kernel(norm_ref, both_ref, coupled_ref, left_ref, right_ref, source_ref, dens_ref, held_ref):
    held_ref[0] = coupled_ref[...]
    held_ref[1] = both_ref[0]
    dens_ref[...] = both_ref[0]

    def turn_step(turn, _):
        real = time_step * (both_ref[1, 1] + field_weight * dens_ref[1])
        imag = -time_step * (both_ref[1, 0] + field_weight * dens_ref[0])
        rh, rl = split_in_kernel(real)
        ih, il = split_in_kernel(imag)
        upper = [rh, -ih, rh, -ih, rl, -il]
        lower = [ih, rh, ih, rh, il, rl]
        left_ref[turn] = jnp.concatenate(
            [jnp.concatenate(upper, axis=1), jnp.concatenate(lower, axis=1)], axis=0
        )
        first_columns = [rh, -ih, rh, -ih, rl, -il]
        last_columns = [ih, rh, ih, rh, il, rl]
        right_ref[turn] = jnp.concatenate(
            [jnp.concatenate(first_columns, axis=0), jnp.concatenate(last_columns, axis=0)], axis=1
        )
        first, second = turn == 0, turn == 1
        kept = jnp.where(first, 1.0, 0.0)
        scale = jnp.where(first, 0.0, jnp.where(second, time_step, 1.0))
        added = jnp.where(second, time_step, 0.0)

        def apply(which, _):
            real, imag = step_of(held_ref[which, 0], held_ref[which, 1], left_ref[turn], right_ref[turn])
            chain = which == 0
            keep = jnp.where(chain, 0.0, kept)
            take = jnp.where(chain, 1.0, scale)
            more = jnp.where(chain, time_step * norm_ref[0], added)
            held_ref[which, 0] = keep * held_ref[which, 0] + take * real + more * dens_ref[0]
            held_ref[which, 1] = keep * held_ref[which, 1] + take * imag + more * dens_ref[1]
            return 0

        lax.fori_loop(0, 2, apply, 0)
        grown = jnp.where(turn < 2, time_step, 0.0)
        dens_ref[...] = dens_ref[...] + grown * held_ref[0]
        return 0

    lax.fori_loop(0, 3, turn_step, 0)
    source_ref[...] = held_ref[1]


def tables(norm, both, coupled):
    order = coupled.shape[-1]
    whole = pl.BlockSpec(memory_space=pltpu.VMEM)
    matrix = jax.ShapeDtypeStruct((2, order, order), jnp.float32)
    return pl.pallas_call(
        densities_kernel,
        out_shape=(
            jax.ShapeDtypeStruct((3, 2 * order, 6 * order), jnp.bfloat16),
            jax.ShapeDtypeStruct((3, 6 * order, 2 * order), jnp.bfloat16),
            matrix,
            matrix,
        ),
        in_specs=[pl.BlockSpec(memory_space=pltpu.SMEM), whole, whole],
        out_specs=(whole,) * 4,
        scratch_shapes=[pltpu.VMEM((2, 2, order, order), jnp.float32)],
        name="densities",
    )(norm, both, coupled)


def on_device(correlators, density, bare_hamiltonian, coupling, propagator):
    local, _, rows, order = correlators.shape
    groups, rings = lax.axis_size("mode"), lax.axis_size("orb")
    place, ring = lax.axis_index("mode"), lax.axis_index("orb")
    modes = local * groups
    owned = local // rings
    depth = 2 * rows // groups

    flat = correlators.reshape(local, 2 * rows, order)
    deep, wide = depth // tile_rows, order // tile_cols
    blocks = [(b, h) for b in range(deep) for h in range(wide)]
    here = place.reshape(1)

    mine = jnp.concatenate(
        [propagator, jnp.zeros((tile_rows, modes), jnp.float32).at[0, :local].set(coupling)]
    )
    even = [swap(mine, "mode", k) if k else mine for k in range(0, groups, 2)]
    odd = swap(jnp.stack(even), "mode", 1)
    gathered = by_place(
        [part for j in range(groups // 2) for part in (even[j], odd[j])], place
    )
    weights = gathered[:, local, :local].reshape(modes)
    full = gathered[:, :local].reshape(modes, modes)
    mixed_weights = contract("m,mn->n", weights, full)
    norm = jnp.sum(weights * weights)
    norm_mixed = jnp.sum(mixed_weights * weights)
    rows16 = jnp.zeros((2 * tile_rows, modes), jnp.float32).at[0].set(mixed_weights)
    high, low = split(jnp.concatenate([full, rows16]))

    near = place & 1
    small = jnp.stack([density, bare_hamiltonian])
    small = lax.dynamic_slice_in_dim(small, near * (rows // 2), rows // 2, 2)
    small = exchange([small] * rings, "orb")

    share = rows // groups
    count = len(blocks)
    packed = [pack(here, flat, groups, depth, *blocks[0])]
    packed.append(pack(here, after(flat, packed[0][0]), groups, depth, *blocks[1]))
    wholes, sums, mixes = [], {}, []
    for turn, (b, h) in enumerate(blocks):
        pieces = exchange([piece.reshape(-1, tile_cols) for piece in packed[turn]], "mode")
        ready = after(here, wholes[turn - 2]) if turn > 1 else here
        mixed, sums[b, h] = mix(ready, high, low, pieces)
        mixes.append(mixed)
        mixed = mixed.reshape(groups * rings, owned * tile_rows, tile_cols)
        wholes.append(lax.all_to_all(mixed, ("mode", "orb"), 0, 0, tiled=True))
        if turn + 2 < count:
            ready = after(flat, wholes[turn - 1] if turn else mixes[0])
            packed.append(pack(here, ready, groups, depth, *blocks[turn + 2]))
        if turn == 0:
            reached = (mixes[0], packed[2][0])
            coupled = jnp.sum(coupling[:, None, None, None] * after(correlators, reached), axis=0)
            coupled = [
                lax.dynamic_slice_in_dim(coupled, (place ^ k) * share, share, 1)
                for k in range(groups)
            ]
            coupled = exchange(coupled, "mode")
        if turn == 1:
            reached = (wholes[0], packed[3][0])
            coupled = sum(after(tuple(coupled), reached))
            coupled = exchange([coupled] * rings, "orb")
            small = by_place(after(tuple(small), reached), ring)
            other = swap(small, "mode", 1)
        if turn == 2:
            coupled = by_place(after(tuple(coupled), wholes[1]), ring)
            coupled = exchange([coupled] * groups, "mode")
            other = after(other, wholes[1])
            both = jnp.stack(
                [jnp.where(near == 1, other, small), jnp.where(near == 1, small, other)], axis=3
            )
            both = jnp.moveaxis(both, 0, 2).reshape(2, 2, order, order)
        if turn == 3:
            coupled = by_place(after(tuple(coupled), wholes[2]), place)
    coupled = coupled.transpose(2, 1, 0, 3, 4).reshape(2, order, order)
    left, right, source, dens2 = tables(norm.reshape(1), both, coupled)
    own_coupling = lax.dynamic_slice_in_dim(coupling, ring * owned, owned, 0)
    own_rows = lax.dynamic_slice_in_dim(propagator, ring * owned, owned, 0)
    scales = jnp.stack([contract("mn,n->m", own_rows, weights), time_step * own_coupling])

    stacks = jnp.zeros(correlators.shape, jnp.float32)
    first, finished = 0, []
    for share in out_shares:
        chunk = share * owned // sum(out_shares)
        parts = steps(
            ring.reshape(1), scales[:, first : first + chunk], left, right, source, dens2,
            wholes, blocks, groups, rings, first, chunk,
        )
        finished.append(parts[0])
        for k, part in enumerate(parts):
            part = swap(part, "orb", k) if k else part
            stacks = lax.dynamic_update_slice(stacks, part, ((ring ^ k) * owned + first, 0, 0, 0))
        first += chunk

    summed = jnp.stack([sums[block] for block in blocks])
    summed = gather_by_doubling(after(summed, finished[0]), "orb")
    summed = gather_by_doubling(after(summed, finished[-1]), "mode")
    summed = summed.reshape((groups * rings,) + summed.shape[2:])
    scales = jnp.stack([norm_mixed, time_step * norm]).reshape(2, 1)
    parts = steps(
        ring.reshape(1), scales, left, right, source, dens2,
        [summed[:, k] for k in range(len(blocks))], blocks, groups, rings, 0, 1,
    )
    dens = lax.dynamic_slice_in_dim(dens2, ring * rows, rows, 1) + time_step * parts[0][0]
    return stacks, dens


def on_device_plain(correlators, density, bare_hamiltonian, coupling, propagator):
    local, _, rows, order = correlators.shape
    groups, rings = lax.axis_size("mode"), lax.axis_size("orb")
    ring = lax.axis_index("orb")
    owned = local // rings
    full = lax.all_gather(propagator, "mode", axis=0, tiled=True)
    weights = lax.all_gather(coupling, "mode", axis=0, tiled=True)
    mixed_weights = contract("m,mn->n", weights, full)
    norm, norm_mixed = jnp.sum(weights * weights), jnp.sum(mixed_weights * weights)
    both = lax.all_gather(jnp.stack([density, bare_hamiltonian]), "orb", axis=2, tiled=True)
    sums = jnp.stack(
        [
            contract("m,mcij->cij", coupling, correlators),
            contract(
                "m,mcij->cij",
                lax.dynamic_slice_in_dim(mixed_weights, lax.axis_index("mode") * local, local, 0),
                correlators,
            ),
        ]
    )
    sums = lax.all_gather(lax.psum(sums, "mode"), "orb", axis=2, tiled=True)
    gens, dens2, source = densities(both[0], both[1], sums[0], norm)
    entries = lax.all_to_all(correlators.reshape(local, groups, -1), "mode", 1, 0, tiled=True)
    mixed = contract("mn,nx->mx", full, entries.reshape(full.shape[0], -1))
    mixed = lax.all_to_all(mixed.reshape(groups * rings, -1), ("mode", "orb"), 0, 0, tiled=True)
    whole = mixed.reshape(groups, rings, owned, -1).transpose(2, 1, 0, 3)
    whole = whole.reshape(owned, rings, 2, rows, order).transpose(0, 2, 1, 3, 4)
    whole = whole.reshape(owned, 2, order, order)
    for gen in gens:
        whole = jax.vmap(lambda matrix, gen=gen: apply_step(gen, matrix))(whole)
    own_coupling = lax.dynamic_slice_in_dim(coupling, ring * owned, owned, 0)
    own_rows = lax.dynamic_slice_in_dim(propagator, ring * owned, owned, 0)
    scale = contract("mn,n->m", own_rows, weights)
    whole = (
        whole
        + scale[:, None, None, None] * source[None]
        + time_step * own_coupling[:, None, None, None] * dens2[None]
    )
    stacks = lax.all_to_all(whole, "orb", split_axis=2, concat_axis=0, tiled=True)
    dens = last_density(gens, dens2, source, sums[1], norm, norm_mixed)
    return stacks, lax.dynamic_slice_in_dim(dens, ring * rows, rows, 1)


def solution(mesh):
    in_specs = (
        P("mode", None, "orb", None),
        P(None, "orb", None),
        P(None, "orb", None),
        P("mode"),
        P("mode", None),
    )
    out_specs = (P("mode", None, "orb", None), P(None, "orb", None))
    groups, rings = mesh.shape["mode"], mesh.shape["orb"]

    def body(correlators, *others):
        local, _, rows, order = correlators.shape
        fits = (
            groups > 1
            and groups & (groups - 1) == 0
            and rings & (rings - 1) == 0
            and rows % (groups * tile_rows) == 0
            and order % tile_cols == 0
            and 2 * rows * order >= 4 * groups * tile_rows * tile_cols
            and local % (2 * tile_rows) == 0
            and local % (rings * sum(out_shares)) == 0
        )
        return (on_device if fits else on_device_plain)(correlators, *others)

    return jax.shard_map(
        body, mesh=mesh, in_specs=in_specs, out_specs=out_specs, check_vma=False
    )
```

```python
import jax
import jax.numpy as jnp
from jax import lax
from jax.experimental import pallas as pl
from jax.experimental.pallas import tpu as pltpu
from jax.sharding import PartitionSpec as P

time_step = 0.1
field_weight = 0.0625
tile_rows, tile_cols = 8, 128
out_shares = (2, 3, 5, 6)


def contract(form, first, second):
    return jnp.einsum(form, first, second, precision=lax.Precision.HIGHEST)


def embed(matrix):
    real, imag = matrix[0], matrix[1]
    return jnp.concatenate(
        [jnp.concatenate([real, -imag], axis=1), jnp.concatenate([imag, real], axis=1)], axis=0
    )


def product(first, second):
    flat = second.reshape(-1, second.shape[-1])
    return contract("ij,jk->ik", embed(first), flat).reshape(second.shape)


def generator(hamil):
    return jnp.stack([time_step * hamil[1], -time_step * hamil[0]])


def apply_step(gen, matrix):
    return matrix + product(gen, matrix) - product(matrix, gen)


def split(values):
    high = lax.reduce_precision(values, exponent_bits=8, mantissa_bits=7)
    return high.astype(jnp.bfloat16), (values - high).astype(jnp.bfloat16)


def split_in_kernel(values):
    high = values.astype(jnp.bfloat16)
    return high, (values - high.astype(jnp.float32)).astype(jnp.bfloat16)


def dot(first, second):
    return jnp.dot(first, second, preferred_element_type=jnp.float32)


def densities(dens, bare, coupled, norm):
    gen0 = generator(bare + field_weight * dens)
    coupled1 = apply_step(gen0, coupled) + time_step * norm * dens
    dens1 = dens + time_step * coupled1
    gen1 = generator(bare + field_weight * dens1)
    coupled2 = apply_step(gen1, coupled1) + time_step * norm * dens1
    dens2 = dens1 + time_step * coupled2
    gen2 = generator(bare + field_weight * dens2)
    source = apply_step(gen2, time_step * (apply_step(gen1, dens) + dens1))
    return (gen0, gen1, gen2), dens2, source


def last_density(gens, dens2, source, coupled_mixed, norm, norm_mixed):
    value = coupled_mixed
    for gen in gens:
        value = apply_step(gen, value)
    return dens2 + time_step * (value + norm_mixed * source + time_step * norm * dens2)


def swap(array, axis, offset):
    return lax.ppermute(array, axis, [(i, i ^ offset) for i in range(lax.axis_size(axis))])


def gather_by_doubling(array, axis):
    place = lax.axis_index(axis)
    offset, done, current = lax.axis_size(axis) // 2, 0, array
    while offset:
        other = swap(current, axis, offset)
        upper = (place & offset) != 0
        current = jnp.stack(
            [jnp.where(upper, other, current), jnp.where(upper, current, other)], axis=done
        )
        done, offset = done + 1, offset // 2
    return current.reshape((-1,) + array.shape)


def exchange(pieces, axis):
    return [swap(piece, axis, k) if k else piece for k, piece in enumerate(pieces)]


def by_place(received, place):
    current, offset = jnp.stack(received), 1
    while offset < len(received):
        pairs = current.reshape((-1, 2, offset) + received[0].shape)
        turned = jnp.concatenate([pairs[:, 1:], pairs[:, :1]], axis=1)
        current = jnp.where((place & offset) != 0, turned, pairs)
        offset *= 2
    return current.reshape((len(received),) + received[0].shape)


def after(array, other):
    return lax.optimization_barrier((array, other))[0]


def pack_kernel(depth, b, h, place_ref, flat_ref, *refs):
    outs, (held_ref, into, back) = refs[:-3], refs[-3:]
    fetched, stored = [], []
    for k, out in enumerate(outs):
        row = pl.multiple_of((place_ref[0] ^ k) * depth + b * tile_rows, tile_rows)
        source = flat_ref.at[:, pl.ds(row, tile_rows), h * tile_cols : (h + 1) * tile_cols]
        fetched.append(pltpu.make_async_copy(source, held_ref.at[k], into.at[k]))
        stored.append(pltpu.make_async_copy(held_ref.at[k], out, back.at[k]))
        fetched[-1].start()
    for fetch, store in zip(fetched, stored):
        fetch.wait()
        store.start()
    for store in stored:
        store.wait()


def pack(place, flat, groups, depth, b, h):
    piece = jax.ShapeDtypeStruct((flat.shape[0], tile_rows, tile_cols), jnp.float32)
    return pl.pallas_call(
        lambda *refs: pack_kernel(depth, b, h, *refs),
        out_shape=(piece,) * groups,
        in_specs=[pl.BlockSpec(memory_space=pltpu.SMEM), pl.BlockSpec(memory_space=pl.ANY)],
        out_specs=(pl.BlockSpec(memory_space=pl.ANY),) * groups,
        scratch_shapes=[
            pltpu.VMEM((groups,) + piece.shape, jnp.float32),
            pltpu.SemaphoreType.DMA((groups,)),
            pltpu.SemaphoreType.DMA((groups,)),
        ],
        name="pack",
    )(place, flat)


def mix_kernel(place_ref, high_ref, low_ref, *refs):
    groups = len(refs) - 4
    pieces, (out_ref, sum_ref, xh_ref, xl_ref) = refs[:groups], refs[groups:]
    place = place_ref[0]
    count = pieces[0].shape[0] // tile_rows
    modes = groups * count
    for k, piece in enumerate(pieces):
        base = pl.multiple_of((place ^ k) * count, count)
        for q in range(tile_rows):
            high, low = split_in_kernel(piece[pl.ds(q, count, stride=tile_rows), :])
            xh_ref[pl.ds(base, count), q * tile_cols : (q + 1) * tile_cols] = high
            xl_ref[pl.ds(base, count), q * tile_cols : (q + 1) * tile_cols] = low
    xh, xl = xh_ref[...], xl_ref[...]
    mixed = dot(high_ref[...], xh) + dot(high_ref[...], xl) + dot(low_ref[...], xh)
    for q in range(tile_rows):
        part = mixed[:, q * tile_cols : (q + 1) * tile_cols]
        out_ref[pl.ds(q, modes, stride=tile_rows), :] = part[:modes]
        sum_ref[q : q + 1, :] = part[modes : modes + 1]


def mix(place, high, low, pieces):
    groups, length = len(pieces), pieces[0].shape[0]
    modes = groups * length // tile_rows
    return pl.pallas_call(
        mix_kernel,
        out_shape=(
            jax.ShapeDtypeStruct((groups * length, tile_cols), jnp.float32),
            jax.ShapeDtypeStruct((tile_rows, tile_cols), jnp.float32),
        ),
        in_specs=[pl.BlockSpec(memory_space=pltpu.SMEM)]
        + [pl.BlockSpec(memory_space=pltpu.VMEM)] * (2 + groups),
        out_specs=(
            pl.BlockSpec(memory_space=pltpu.VMEM),
            pl.BlockSpec(memory_space=pltpu.VMEM),
        ),
        scratch_shapes=[
            pltpu.VMEM((modes, tile_rows * tile_cols), jnp.bfloat16),
            pltpu.VMEM((modes, tile_rows * tile_cols), jnp.bfloat16),
        ],
        name="mix",
    )(place, high, low, *pieces)


def step_of(real, imag, left, right):
    order = real.shape[-1]
    rh, rl = split_in_kernel(real)
    ih, il = split_in_kernel(imag)
    before = dot(left, jnp.concatenate([rh, ih, rl, il, rh, ih], axis=0))
    behind = dot(jnp.concatenate([rh, ih, rl, il, rh, ih], axis=1), right)
    return (
        real + (before[:order] - behind[:, :order]),
        imag + (before[order:] - behind[:, order:]),
    )


def steps_kernel(groups, rings, blocks, place_ref, scale_ref, left_ref, right_ref, source_ref, dens_ref, *refs):
    pieces, outs = refs[: len(blocks)], refs[len(blocks) : -4]
    g_ref, left_held, right_held, sem = refs[-4:]
    order = g_ref.shape[-1]
    rows = order // rings
    half = groups // 2
    deep = 1 + max(b for b, _ in blocks)
    turns = left_ref.shape[0]
    m = pl.program_id(0)

    def fetch(turn):
        return (
            pltpu.make_async_copy(left_ref.at[turn], left_held.at[turn], sem.at[turn, 0]),
            pltpu.make_async_copy(right_ref.at[turn], right_held.at[turn], sem.at[turn, 1]),
        )

    @pl.when(m == 0)
    def _():
        for turn in range(turns):
            for copy in fetch(turn):
                copy.start()

    for piece, (b, h) in zip(pieces, blocks):
        for c in range(2):
            for d in range(half):
                for z in range(rings):
                    row = z * rows + (d * deep + b) * tile_rows
                    g_ref[c, row : row + tile_rows, h * tile_cols : (h + 1) * tile_cols] = piece[
                        (c * half + d) * rings + z
                    ]

    def turn_step(turn, _):
        @pl.when(m == 0)
        def _():
            for copy in fetch(turn):
                copy.wait()

        real, imag = step_of(g_ref[0], g_ref[1], left_held[turn], right_held[turn])
        g_ref[0] = real
        g_ref[1] = imag
        return 0

    lax.fori_loop(0, turns, turn_step, 0)
    mixed, own = scale_ref[0, m], scale_ref[1, m]
    g_ref[...] = g_ref[...] + mixed * source_ref[...] + own * dens_ref[...]
    place = place_ref[0]
    for k, out in enumerate(outs):
        base = pl.multiple_of((place ^ k) * rows, rows)
        out[0] = g_ref[:, pl.ds(base, rows), :]


def steps(place, scales, left, right, source, dens, pieces, blocks, groups, rings, first, count):
    order = dens.shape[-1]
    rows = order // rings
    whole = pl.BlockSpec(memory_space=pltpu.VMEM)
    table = pl.BlockSpec(memory_space=pltpu.SMEM)
    apart = pl.BlockSpec(memory_space=pl.ANY)
    return pl.pallas_call(
        lambda *refs: steps_kernel(groups, rings, blocks, *refs),
        grid=(count,),
        out_shape=tuple(
            jax.ShapeDtypeStruct((count, 2, rows, order), jnp.float32) for _ in range(rings)
        ),
        in_specs=[table, table, apart, apart, whole, whole]
        + [
            pl.BlockSpec((groups * rings, tile_rows, tile_cols), lambda m: (0, first + m, 0))
            for _ in pieces
        ],
        out_specs=tuple(
            pl.BlockSpec((1, 2, rows, order), lambda m: (m, 0, 0, 0)) for _ in range(rings)
        ),
        scratch_shapes=[
            pltpu.VMEM((2, order, order), jnp.float32),
            pltpu.VMEM(left.shape, left.dtype),
            pltpu.VMEM(right.shape, right.dtype),
            pltpu.SemaphoreType.DMA((left.shape[0], 2)),
        ],
        name="steps",
    )(place, scales, left, right, source, dens, *pieces)


def densities_kernel(norm_ref, both_ref, coupled_ref, left_ref, right_ref, source_ref, dens_ref, held_ref):
    held_ref[0] = coupled_ref[...]
    held_ref[1] = both_ref[0]
    dens_ref[...] = both_ref[0]

    def turn_step(turn, _):
        real = time_step * (both_ref[1, 1] + field_weight * dens_ref[1])
        imag = -time_step * (both_ref[1, 0] + field_weight * dens_ref[0])
        rh, rl = split_in_kernel(real)
        ih, il = split_in_kernel(imag)
        upper = [rh, -ih, rh, -ih, rl, -il]
        lower = [ih, rh, ih, rh, il, rl]
        left_ref[turn] = jnp.concatenate(
            [jnp.concatenate(upper, axis=1), jnp.concatenate(lower, axis=1)], axis=0
        )
        first_columns = [rh, -ih, rh, -ih, rl, -il]
        last_columns = [ih, rh, ih, rh, il, rl]
        right_ref[turn] = jnp.concatenate(
            [jnp.concatenate(first_columns, axis=0), jnp.concatenate(last_columns, axis=0)], axis=1
        )
        first, second = turn == 0, turn == 1
        kept = jnp.where(first, 1.0, 0.0)
        scale = jnp.where(first, 0.0, jnp.where(second, time_step, 1.0))
        added = jnp.where(second, time_step, 0.0)

        def apply(which, _):
            real, imag = step_of(held_ref[which, 0], held_ref[which, 1], left_ref[turn], right_ref[turn])
            chain = which == 0
            keep = jnp.where(chain, 0.0, kept)
            take = jnp.where(chain, 1.0, scale)
            more = jnp.where(chain, time_step * norm_ref[0], added)
            held_ref[which, 0] = keep * held_ref[which, 0] + take * real + more * dens_ref[0]
            held_ref[which, 1] = keep * held_ref[which, 1] + take * imag + more * dens_ref[1]
            return 0

        lax.fori_loop(0, 2, apply, 0)
        grown = jnp.where(turn < 2, time_step, 0.0)
        dens_ref[...] = dens_ref[...] + grown * held_ref[0]
        return 0

    lax.fori_loop(0, 3, turn_step, 0)
    source_ref[...] = held_ref[1]


def tables(norm, both, coupled):
    order = coupled.shape[-1]
    whole = pl.BlockSpec(memory_space=pltpu.VMEM)
    matrix = jax.ShapeDtypeStruct((2, order, order), jnp.float32)
    return pl.pallas_call(
        densities_kernel,
        out_shape=(
            jax.ShapeDtypeStruct((3, 2 * order, 6 * order), jnp.bfloat16),
            jax.ShapeDtypeStruct((3, 6 * order, 2 * order), jnp.bfloat16),
            matrix,
            matrix,
        ),
        in_specs=[pl.BlockSpec(memory_space=pltpu.SMEM), whole, whole],
        out_specs=(whole,) * 4,
        scratch_shapes=[pltpu.VMEM((2, 2, order, order), jnp.float32)],
        name="densities",
    )(norm, both, coupled)


def on_device(correlators, density, bare_hamiltonian, coupling, propagator):
    local, _, rows, order = correlators.shape
    groups, rings = lax.axis_size("mode"), lax.axis_size("orb")
    place, ring = lax.axis_index("mode"), lax.axis_index("orb")
    modes = local * groups
    owned = local // rings
    depth = 2 * rows // groups

    flat = correlators.reshape(local, 2 * rows, order)
    deep, wide = depth // tile_rows, order // tile_cols
    blocks = [(b, h) for b in range(deep) for h in range(wide)]
    here = place.reshape(1)

    mine = jnp.concatenate(
        [propagator, jnp.zeros((tile_rows, modes), jnp.float32).at[0, :local].set(coupling)]
    )
    even = [swap(mine, "mode", k) if k else mine for k in range(0, groups, 2)]
    odd = swap(jnp.stack(even), "mode", 1)
    gathered = by_place(
        [part for j in range(groups // 2) for part in (even[j], odd[j])], place
    )
    weights = gathered[:, local, :local].reshape(modes)
    full = gathered[:, :local].reshape(modes, modes)
    mixed_weights = contract("m,mn->n", weights, full)
    norm = jnp.sum(weights * weights)
    norm_mixed = jnp.sum(mixed_weights * weights)
    rows16 = jnp.zeros((2 * tile_rows, modes), jnp.float32).at[0].set(mixed_weights)
    high, low = split(jnp.concatenate([full, rows16]))

    near = place & 1
    small = jnp.stack([density, bare_hamiltonian])
    small = lax.dynamic_slice_in_dim(small, near * (rows // 2), rows // 2, 2)
    small = exchange([small] * rings, "orb")

    share = rows // groups
    count = len(blocks)
    packed = [pack(here, flat, groups, depth, *blocks[0])]
    packed.append(pack(here, after(flat, (packed[0][0], high)), groups, depth, *blocks[1]))
    wholes, sums, mixes = [], {}, []
    for turn, (b, h) in enumerate(blocks):
        pieces = exchange([piece.reshape(-1, tile_cols) for piece in packed[turn]], "mode")
        ready = after(here, wholes[turn - 2]) if turn > 1 else here
        mixed, sums[b, h] = mix(ready, high, low, pieces)
        mixes.append(mixed)
        mixed = mixed.reshape(groups * rings, owned * tile_rows, tile_cols)
        wholes.append(lax.all_to_all(mixed, ("mode", "orb"), 0, 0, tiled=True))
        if turn + 2 < count:
            ready = after(flat, wholes[turn - 1] if turn else mixes[0])
            packed.append(pack(here, ready, groups, depth, *blocks[turn + 2]))
        if turn == 0:
            reached = (mixes[0], packed[2][0])
            coupled = jnp.sum(coupling[:, None, None, None] * after(correlators, reached), axis=0)
            coupled = [
                lax.dynamic_slice_in_dim(coupled, (place ^ k) * share, share, 1)
                for k in range(groups)
            ]
            coupled = exchange(coupled, "mode")
        if turn == 1:
            reached = (wholes[0], packed[3][0])
            coupled = sum(after(tuple(coupled), reached))
            coupled = exchange([coupled] * rings, "orb")
            small = by_place(after(tuple(small), reached), ring)
            other = swap(small, "mode", 1)
        if turn == 2:
            coupled = by_place(after(tuple(coupled), wholes[1]), ring)
            coupled = exchange([coupled] * groups, "mode")
            other = after(other, wholes[1])
            both = jnp.stack(
                [jnp.where(near == 1, other, small), jnp.where(near == 1, small, other)], axis=3
            )
            both = jnp.moveaxis(both, 0, 2).reshape(2, 2, order, order)
        if turn == 3:
            coupled = by_place(after(tuple(coupled), wholes[2]), place)
    summed = jnp.stack([sums[block] for block in blocks])
    summed = tuple(exchange([summed] * rings, "orb"))
    coupled = coupled.transpose(2, 1, 0, 3, 4).reshape(2, order, order)
    left, right, source, dens2 = tables(norm.reshape(1), both, coupled)
    own_coupling = lax.dynamic_slice_in_dim(coupling, ring * owned, owned, 0)
    own_rows = lax.dynamic_slice_in_dim(propagator, ring * owned, owned, 0)
    scales = jnp.stack([contract("mn,n->m", own_rows, weights), time_step * own_coupling])

    stacks = jnp.zeros(correlators.shape, jnp.float32)
    first, finished = 0, []
    for share in out_shares:
        chunk = share * owned // sum(out_shares)
        turn = ring.reshape(1)
        parts = steps(
            after(turn, finished[-1]) if finished else turn, scales[:, first : first + chunk],
            left, right, source, dens2, wholes, blocks, groups, rings, first, chunk,
        )
        finished.append(parts[0])
        parts = exchange(parts, "orb")
        for k, part in enumerate(parts):
            stacks = lax.dynamic_update_slice(stacks, part, ((ring ^ k) * owned + first, 0, 0, 0))
        first += chunk

    summed = by_place(after(summed, finished[-1]), ring)
    summed = gather_by_doubling(summed, "mode")
    summed = summed.reshape((groups * rings,) + summed.shape[2:])
    scales = jnp.stack([norm_mixed, time_step * norm]).reshape(2, 1)
    parts = steps(
        ring.reshape(1), scales, left, right, source, dens2,
        [summed[:, k] for k in range(len(blocks))], blocks, groups, rings, 0, 1,
    )
    dens = lax.dynamic_slice_in_dim(dens2, ring * rows, rows, 1) + time_step * parts[0][0]
    return stacks, dens


def on_device_plain(correlators, density, bare_hamiltonian, coupling, propagator):
    local, _, rows, order = correlators.shape
    groups, rings = lax.axis_size("mode"), lax.axis_size("orb")
    ring = lax.axis_index("orb")
    owned = local // rings
    full = lax.all_gather(propagator, "mode", axis=0, tiled=True)
    weights = lax.all_gather(coupling, "mode", axis=0, tiled=True)
    mixed_weights = contract("m,mn->n", weights, full)
    norm, norm_mixed = jnp.sum(weights * weights), jnp.sum(mixed_weights * weights)
    both = lax.all_gather(jnp.stack([density, bare_hamiltonian]), "orb", axis=2, tiled=True)
    sums = jnp.stack(
        [
            contract("m,mcij->cij", coupling, correlators),
            contract(
                "m,mcij->cij",
                lax.dynamic_slice_in_dim(mixed_weights, lax.axis_index("mode") * local, local, 0),
                correlators,
            ),
        ]
    )
    sums = lax.all_gather(lax.psum(sums, "mode"), "orb", axis=2, tiled=True)
    gens, dens2, source = densities(both[0], both[1], sums[0], norm)
    entries = lax.all_to_all(correlators.reshape(local, groups, -1), "mode", 1, 0, tiled=True)
    mixed = contract("mn,nx->mx", full, entries.reshape(full.shape[0], -1))
    mixed = lax.all_to_all(mixed.reshape(groups * rings, -1), ("mode", "orb"), 0, 0, tiled=True)
    whole = mixed.reshape(groups, rings, owned, -1).transpose(2, 1, 0, 3)
    whole = whole.reshape(owned, rings, 2, rows, order).transpose(0, 2, 1, 3, 4)
    whole = whole.reshape(owned, 2, order, order)
    for gen in gens:
        whole = jax.vmap(lambda matrix, gen=gen: apply_step(gen, matrix))(whole)
    own_coupling = lax.dynamic_slice_in_dim(coupling, ring * owned, owned, 0)
    own_rows = lax.dynamic_slice_in_dim(propagator, ring * owned, owned, 0)
    scale = contract("mn,n->m", own_rows, weights)
    whole = (
        whole
        + scale[:, None, None, None] * source[None]
        + time_step * own_coupling[:, None, None, None] * dens2[None]
    )
    stacks = lax.all_to_all(whole, "orb", split_axis=2, concat_axis=0, tiled=True)
    dens = last_density(gens, dens2, source, sums[1], norm, norm_mixed)
    return stacks, lax.dynamic_slice_in_dim(dens, ring * rows, rows, 1)


def solution(mesh):
    in_specs = (
        P("mode", None, "orb", None),
        P(None, "orb", None),
        P(None, "orb", None),
        P("mode"),
        P("mode", None),
    )
    out_specs = (P("mode", None, "orb", None), P(None, "orb", None))
    groups, rings = mesh.shape["mode"], mesh.shape["orb"]

    def body(correlators, *others):
        local, _, rows, order = correlators.shape
        fits = (
            groups > 1
            and groups & (groups - 1) == 0
            and rings & (rings - 1) == 0
            and rows % (groups * tile_rows) == 0
            and order % tile_cols == 0
            and 2 * rows * order >= 4 * groups * tile_rows * tile_cols
            and local % (2 * tile_rows) == 0
            and local % (rings * sum(out_shares)) == 0
        )
        return (on_device if fits else on_device_plain)(correlators, *others)

    return jax.shard_map(
        body, mesh=mesh, in_specs=in_specs, out_specs=out_specs, check_vma=False
    )
```
